32 devices in a mesh: seq: 8 (over y, x, core), ch: 4 (over z).
Axes of the slice: x: 2, y: 2, z: 4, core: 2. Of those that a mesh axis runs over, the one named last changes fastest.
Arguments:
- signal: bfloat16 [1024, 128, 1024], P('seq', 'ch'), may hold values from -6 to 6
- cotangent: bfloat16 [1024, 128, 1024], P('seq', 'ch'), may hold values from -6 to 6
- right_factor: bfloat16 [1024, 1024], replicated, may hold values from -0.1875 to 0.1875
- left_factor: bfloat16 [1024, 1024], replicated, may hold values from -0.1875 to 0.1875
- right_blocks: int32 [8, 8], replicated, may hold values 0 or 1
- left_blocks: int32 [8, 8], replicated, may hold values 0 or 1
Outputs:
- mixed: bfloat16 [1024, 128, 1024], P('seq', 'ch')
- grad_signal: bfloat16 [1024, 128, 1024], P('seq', 'ch')
- grad_right: float32 [1024, 1024], P('seq', 'ch')
- grad_left: float32 [1024, 1024], P('seq', 'ch')
The draws below stay inside these ranges and needn't reach their ends.
All inputs are finite; a program needn't handle non-finite values.
Results may differ from the reference program's by a relative error of at most 0.0051.
Values may be sent and summed in bfloat16 or wider, within the bound.
A program may use at most 192 MiB of HBM per device.

```python
import math
import jax
import jax.numpy as jnp
from jax import lax

M1 = 1024
M2 = 1024
C = 128
MB1 = 8
MB2 = 8


def touch_ends(values, own_key, low, high):
    spot = [jax.random.randint(jax.random.fold_in(own_key, axis), (), 0, length) for axis, length in enumerate(values.shape)]
    widest = values.shape.index(max(values.shape))
    beside = spot[:widest] + [(spot[widest] + 1) % values.shape[widest]] + spot[widest + 1:]
    return values.at[tuple(spot)].set(low).at[tuple(beside)].set(high)


def levels(own_key, extent, cuts, least, top_value):
    gain, own = 1.0, jax.random.fold_in(own_key, 6)
    for dim, blocks in cuts:
        draws = jnp.exp(jax.random.uniform(jax.random.fold_in(own, dim), (blocks,), jnp.float32, least / len(cuts), top_value / len(cuts)))
        gain = gain * jnp.repeat(draws, extent[dim] // blocks).reshape([-1 if axis == dim else 1 for axis in range(len(extent))])
    return gain


def noise(rng, extent, spread, most, cuts=(), held_as=jnp.bfloat16):
    level = levels(rng, extent, cuts, -0.22, 0.18) if cuts else 1.0
    drawn = jax.random.normal(rng, extent, jnp.float32) * spread * level
    return jnp.minimum(jnp.maximum(drawn, -most), most).astype(held_as)


def setup_inputs(seed: int = 0) -> dict:
    arg_keys = jax.random.split(jax.random.key(seed), 7)
    return {
        "signal": noise(arg_keys[0], (M1, C, M2), 1.0, 6.0, ((0, 8), (1, 4))),
        "cotangent": noise(arg_keys[1], (M1, C, M2), 1.0, 6.0, ((0, 8), (1, 4))),
        "right_factor": noise(arg_keys[2], (M2, M2), M2 ** -0.5, 0.1875),
        "left_factor": noise(arg_keys[3], (M1, M1), M1 ** -0.5, 0.1875),
        "right_blocks": touch_ends((jax.random.randint(arg_keys[4], (MB2, MB2), 0, 8) < 5).astype(jnp.int32), jax.random.fold_in(arg_keys[4], 1), 0, 1),
        "left_blocks": touch_ends((jax.random.randint(arg_keys[5], (MB1, MB1), 0, 8) < 5).astype(jnp.int32), jax.random.fold_in(arg_keys[5], 1), 0, 1),
    }


def expand(blocks, width):
    tile = width // blocks.shape[0]
    return jnp.repeat(jnp.repeat(blocks, tile, axis=0), tile, axis=1)

def reference(signal, cotangent, right_factor, left_factor, right_blocks, left_blocks):
    right_mask = expand(right_blocks, M2).astype(jnp.bfloat16)
    left_mask = expand(left_blocks, M1).astype(jnp.bfloat16)
    right_eff = right_factor * right_mask
    left_eff = left_factor * left_mask
    block = math.gcd(C, 8)
    groups = C // block

    def split(array):
        return array.reshape(M1, groups, block, M2).transpose(1, 0, 2, 3)

    def step(carry, pieces):
        sig, cot = pieces
        flat = sig.reshape(M1 * block, M2)
        z_rows = jnp.dot(flat, right_eff.T, preferred_element_type=jnp.float32).astype(jnp.bfloat16)
        z_cols = z_rows.reshape(M1, block * M2)
        y_val = jnp.dot(left_eff, z_cols, preferred_element_type=jnp.float32).astype(jnp.bfloat16)
        y_val = y_val.reshape(M1, block, M2).astype(jnp.float32)
        sig_f = sig.astype(jnp.float32)
        gate = jax.nn.sigmoid(sig_f)
        swish = sig_f * gate
        mixed = (sig_f + y_val * swish).astype(jnp.bfloat16)
        cot_f = cot.astype(jnp.float32)
        grad_y = (cot_f * swish).astype(jnp.bfloat16)
        grad_cols = grad_y.reshape(M1, block * M2)
        grad_z = jnp.dot(left_eff.T, grad_cols, preferred_element_type=jnp.float32).astype(jnp.bfloat16)
        grad_flat = grad_z.reshape(M1 * block, M2)
        left_term = jnp.dot(grad_cols, z_cols.T, preferred_element_type=jnp.float32)
        right_term = jnp.dot(grad_flat.T, flat, preferred_element_type=jnp.float32)
        back = jnp.dot(grad_flat, right_eff, preferred_element_type=jnp.float32).reshape(M1, block, M2)
        dswish = gate * (1.0 + sig_f * (1.0 - gate))
        grad_sig = (cot_f * (1.0 + y_val * dswish) + back).astype(jnp.bfloat16)
        return ((carry[0] + right_term, carry[1] + left_term), (mixed, grad_sig))
    init = (jnp.zeros((M2, M2), jnp.float32), jnp.zeros((M1, M1), jnp.float32))
    sums, stacked = lax.scan(step, init, (split(signal), split(cotangent)))

    def merge(array):
        return array.transpose(1, 0, 2, 3).reshape(M1, C, M2)
    grad_right = sums[0] * right_mask.astype(jnp.float32) / math.sqrt(M1 * C)
    grad_left = sums[1] * left_mask.astype(jnp.float32) / math.sqrt(M2 * C)
    return (merge(stacked[0]), merge(stacked[1]), grad_right, grad_left)
```

```python
import functools
import math

import jax
import jax.numpy as jnp
from jax import lax
from jax.experimental import pallas as pl
from jax.experimental.pallas import tpu as pltpu
from jax.sharding import PartitionSpec as P


def expand(blocks, width):
    tile = width // blocks.shape[0]
    return jnp.repeat(jnp.repeat(blocks, tile, axis=0), tile, axis=1)


def to_columns(rows, peers):
    rows_here, chans, width_two = rows.shape
    piece = width_two // peers
    arranged = rows.reshape(rows_here, chans, peers, piece).transpose(0, 2, 1, 3)
    return arranged.reshape(rows_here, peers, chans * piece)


def to_rows(received, chans):
    rows_here, peers, wide = received.shape
    piece = wide // chans
    arranged = received.reshape(rows_here, peers, chans, piece).transpose(0, 2, 1, 3)
    return arranged.reshape(rows_here, chans, peers * piece)


def shards_by_column(signal, cotangent, right_factor, left_factor, right_blocks, left_blocks):
    rows_here, chans, width_two = signal.shape
    width_one = left_factor.shape[0]
    peers = lax.axis_size("seq")
    right_mask = expand(right_blocks, width_two).astype(jnp.bfloat16)
    left_mask = expand(left_blocks, width_one).astype(jnp.bfloat16)
    right_eff = right_factor * right_mask
    left_eff = left_factor * left_mask
    flat_signal = signal.reshape(rows_here * chans, width_two)
    first_rows = jnp.dot(flat_signal, right_eff.T, preferred_element_type=jnp.float32)
    first_rows = to_columns(
        first_rows.astype(jnp.bfloat16).reshape(rows_here, chans, width_two), peers
    )
    sig_f = signal.astype(jnp.float32)
    gate = jax.nn.sigmoid(sig_f)
    swish = sig_f * gate
    cot_f = cotangent.astype(jnp.float32)
    grad_rows = to_columns((cot_f * swish).astype(jnp.bfloat16), peers)
    z_cols = lax.all_to_all(first_rows, "seq", split_axis=1, concat_axis=0, tiled=True)
    flat_cols = z_cols.reshape(width_one, z_cols.shape[2])
    result = jnp.dot(left_eff, flat_cols, preferred_element_type=jnp.float32)
    y_cols = result.astype(jnp.bfloat16).reshape(width_one, 1, z_cols.shape[2])
    y_back = lax.all_to_all(y_cols, "seq", split_axis=0, concat_axis=1, tiled=True)
    dy_cols = lax.all_to_all(grad_rows, "seq", split_axis=1, concat_axis=0, tiled=True)
    flat_cols = dy_cols.reshape(width_one, dy_cols.shape[2])
    result = lax.dot_general(
        left_eff, flat_cols, (((0,), (0,)), ((), ())), preferred_element_type=jnp.float32
    )
    dz_cols = result.astype(jnp.bfloat16).reshape(width_one, 1, dy_cols.shape[2])
    dz_back = lax.all_to_all(dz_cols, "seq", split_axis=0, concat_axis=1, tiled=True)
    y_rows = to_rows(y_back, chans)
    dz_rows = to_rows(dz_back, chans)
    y_f = y_rows.astype(jnp.float32)
    mixed = (sig_f + y_f * swish).astype(jnp.bfloat16)
    dz_flat = dz_rows.reshape(rows_here * chans, width_two)
    back = jnp.dot(dz_flat, right_eff, preferred_element_type=jnp.float32).reshape(
        rows_here, chans, width_two
    )
    dswish = gate * (1.0 + sig_f * (1.0 - gate))
    grad_signal = (cot_f * (1.0 + y_f * dswish) + back).astype(jnp.bfloat16)
    wide = z_cols.shape[2]
    z_flat = z_cols.reshape(width_one, wide)
    dy_flat = dy_cols.reshape(width_one, wide)
    left_term = lax.dot_general(
        dy_flat, z_flat, (((1,), (1,)), ((), ())), preferred_element_type=jnp.float32
    )
    right_term = lax.dot_general(
        dz_flat, flat_signal, (((0,), (0,)), ((), ())), preferred_element_type=jnp.float32
    )
    total_chans = chans * lax.axis_size("ch")
    right_term = right_term * right_mask.astype(jnp.float32) / math.sqrt(width_one * total_chans)
    left_term = left_term * left_mask.astype(jnp.float32) / math.sqrt(width_two * total_chans)
    partial_value = (
        lax.psum_scatter(right_term, "seq", scatter_dimension=0, tiled=True),
        lax.psum_scatter(left_term, "seq", scatter_dimension=0, tiled=True),
    )
    grad_right, grad_left = (
        lax.psum_scatter(partial_value[0], "ch", scatter_dimension=1, tiled=True),
        lax.psum_scatter(partial_value[1], "ch", scatter_dimension=1, tiled=True),
    )
    return (mixed, grad_signal, grad_right, grad_left)


def mix_kernel(
    peers, parts, xt, ct, right, left, left_t, mt, gt, grad_r, grad_l,
    xbuf, cbuf, zbuf, dybuf, dzbuf, send_sem, recv_sem, local_sem,
):
    me = lax.axis_index("seq")
    column = lax.axis_index("ch")
    rows = xt.shape[1]
    width = xt.shape[2]
    order = left.shape[0]
    tile = 256

    def own_rows(who):
        return pl.ds(pl.multiple_of(who * rows, rows), rows)

    def far(kind, part, source, target, who):
        return pltpu.make_async_remote_copy(
            src_ref=source,
            dst_ref=target,
            send_sem=send_sem.at[kind, part, who],
            recv_sem=recv_sem.at[kind, part, me],
            device_id=(who, column),
            device_id_type=pl.DeviceIdType.MESH,
        )

    def arrived(kind, part, source, target, who):
        return pltpu.make_async_remote_copy(
            src_ref=source,
            dst_ref=target,
            send_sem=send_sem.at[kind, part, who],
            recv_sem=recv_sem.at[kind, part, who],
            device_id=(who, column),
            device_id_type=pl.DeviceIdType.MESH,
        )

    def each_peer(action):
        @pl.loop(1, peers)
        def _(step):
            action(lax.rem(me + step, peers))

    barrier = pltpu.get_barrier_semaphore()

    def greet(who):
        pl.semaphore_signal(
            barrier, inc=1, device_id=(who, column), device_id_type=pl.DeviceIdType.MESH
        )

    each_peer(greet)
    pl.semaphore_wait(barrier, peers - 1)

    inputs = ((0, xt, xbuf), (1, ct, cbuf))
    outputs = ((2, mt, xbuf), (3, gt, cbuf))

    def send_in(part):
        def one(who):
            for kind, source, held in inputs:
                far(kind, part, source.at[part * peers + who], held.at[part, own_rows(me)], who).start()

        each_peer(one)
        for kind, source, held in inputs:
            pltpu.make_async_copy(
                source.at[part * peers + me], held.at[part, own_rows(me)], local_sem.at[kind, part]
            ).start()

    def wait_in(part):
        def one(who):
            for kind, source, held in inputs:
                arrived(
                    kind, part, source.at[part * peers + who], held.at[part, own_rows(who)], who
                ).wait_recv()

        each_peer(one)
        for kind, source, held in inputs:
            pltpu.make_async_copy(
                source.at[part * peers + me], held.at[part, own_rows(me)], local_sem.at[kind, part]
            ).wait()

    def wait_in_sent(part):
        def one(who):
            for kind, source, held in inputs:
                far(kind, part, source.at[part * peers + who], held.at[part, own_rows(me)], who).wait_send()

        each_peer(one)

    def send_out(part):
        def one(who):
            for kind, target, held in outputs:
                far(kind, part, held.at[part, own_rows(who)], target.at[part * peers + me], who).start()

        each_peer(one)
        for kind, target, held in outputs:
            pltpu.make_async_copy(
                held.at[part, own_rows(me)], target.at[part * peers + me], local_sem.at[kind, part]
            ).start()

    def wait_out(part):
        def one(who):
            for kind, target, held in outputs:
                arrived(
                    kind, part, held.at[part, own_rows(who)], target.at[part * peers + who], who
                ).wait_recv()
                far(kind, part, held.at[part, own_rows(who)], target.at[part * peers + me], who).wait_send()

        each_peer(one)
        for kind, target, held in outputs:
            pltpu.make_async_copy(
                held.at[part, own_rows(me)], target.at[part * peers + me], local_sem.at[kind, part]
            ).wait()

    def at(step):
        return pl.ds(pl.multiple_of(step * tile, tile), tile)

    def dot(a, b, dims):
        return lax.dot_general(a, b, (dims, ((), ())), preferred_element_type=jnp.float32)

    def compute(part):
        @pl.loop(0, order // tile)
        def _(step):
            x = xbuf[part, at(step), :]
            zbuf[at(step), :] = dot(x, right[...], ((1,), (1,))).astype(jnp.bfloat16)
            sig = x.astype(jnp.float32)
            swish = sig * jax.nn.sigmoid(sig)
            cot = cbuf[part, at(step), :].astype(jnp.float32)
            dybuf[at(step), :] = (cot * swish).astype(jnp.bfloat16)

        @pl.loop(0, order // tile)
        def _(step):
            dzbuf[at(step), :] = dot(left_t[at(step), :], dybuf[...], ((1,), (0,))).astype(jnp.bfloat16)
            grad_l[at(step), :] += dot(dybuf[at(step), :], zbuf[...], ((1,), (1,)))

        @pl.loop(0, width // tile)
        def _(step):
            grad_r[at(step), :] += dot(dzbuf[:, at(step)], xbuf[part], ((0,), (0,)))

        @pl.loop(0, order // tile)
        def _(step):
            y = dot(left[at(step), :], zbuf[...], ((1,), (0,))).astype(jnp.bfloat16).astype(jnp.float32)
            back = dot(dzbuf[at(step), :], right[...], ((1,), (0,)))
            sig = xbuf[part, at(step), :].astype(jnp.float32)
            cot = cbuf[part, at(step), :].astype(jnp.float32)
            gate = jax.nn.sigmoid(sig)
            xbuf[part, at(step), :] = (sig + y * (sig * gate)).astype(jnp.bfloat16)
            dswish = gate * (1.0 + sig * (1.0 - gate))
            cbuf[part, at(step), :] = (cot * (1.0 + y * dswish) + back).astype(jnp.bfloat16)

    send_in(0)
    if parts > 1:
        send_in(1)
    grad_r[...] = jnp.zeros_like(grad_r)
    grad_l[...] = jnp.zeros_like(grad_l)

    @pl.loop(0, parts)
    def _(part):
        wait_in(part)

        @pl.when(part + 2 < parts)
        def _():
            send_in(part + 2)

        compute(part)
        send_out(part)

    @pl.loop(0, parts)
    def _(part):
        wait_in_sent(part)
        wait_out(part)


def shards_by_channel(signal, cotangent, right_factor, left_factor, right_blocks, left_blocks):
    rows_here, chans, width_two = signal.shape
    width_one = left_factor.shape[0]
    peers = lax.axis_size("seq")
    groups = lax.axis_size("ch")
    parts = chans // peers
    right_eff = right_factor * expand(right_blocks, width_two).astype(jnp.bfloat16)
    left_eff = left_factor * expand(left_blocks, width_one).astype(jnp.bfloat16)
    xt = signal.transpose(1, 0, 2)
    ct = cotangent.transpose(1, 0, 2)
    hbm = pl.BlockSpec(memory_space=pl.ANY)
    vmem = pl.BlockSpec(memory_space=pltpu.VMEM)
    mt, gt, right_term, left_term = pl.pallas_call(
        functools.partial(mix_kernel, peers, parts),
        out_shape=(
            jax.ShapeDtypeStruct(xt.shape, jnp.bfloat16),
            jax.ShapeDtypeStruct(xt.shape, jnp.bfloat16),
            jax.ShapeDtypeStruct((width_two, width_two), jnp.float32),
            jax.ShapeDtypeStruct((width_one, width_one), jnp.float32),
        ),
        in_specs=[hbm, hbm, vmem, vmem, vmem],
        out_specs=(hbm, hbm, vmem, vmem),
        scratch_shapes=[
            pltpu.VMEM((parts, width_one, width_two), jnp.bfloat16),
            pltpu.VMEM((parts, width_one, width_two), jnp.bfloat16),
            pltpu.VMEM((width_one, width_two), jnp.bfloat16),
            pltpu.VMEM((width_one, width_two), jnp.bfloat16),
            pltpu.VMEM((width_one, width_two), jnp.bfloat16),
            pltpu.SemaphoreType.DMA((4, parts, peers)),
            pltpu.SemaphoreType.DMA((4, parts, peers)),
            pltpu.SemaphoreType.DMA((4, parts)),
        ],
        compiler_params=pltpu.CompilerParams(
            collective_id=0, has_side_effects=True, vmem_limit_bytes=58 * 2**20
        ),
    )(xt, ct, right_eff, left_eff, left_eff.T)
    mixed = mt.transpose(1, 0, 2)
    grad_signal = gt.transpose(1, 0, 2)
    row, col = lax.axis_index("seq"), lax.axis_index("ch")

    def finish(term, blocks, scale):
        term = lax.psum_scatter(term, "ch", scatter_dimension=1, tiled=True)
        term = lax.psum_scatter(term, "seq", scatter_dimension=0, tiled=True)
        mask = expand(blocks, width_two if term.shape[1] * groups == width_two else width_one)
        mask = lax.dynamic_slice(mask, (row * term.shape[0], col * term.shape[1]), term.shape)
        return term * mask.astype(jnp.float32) / scale

    grad_right = finish(right_term, right_blocks, math.sqrt(width_one * chans * groups))
    grad_left = finish(left_term, left_blocks, math.sqrt(width_two * chans * groups))
    return (mixed, grad_signal, grad_right, grad_left)


def shards(signal, *others):
    rows_here, chans, width_two = signal.shape
    peers = lax.axis_size("seq")
    width_one = others[1].shape[0]
    fits = chans % peers == 0 and rows_here % 16 == 0 and peers > 1
    if fits and width_one == 1024 and width_two == 1024 and chans // peers <= 4:
        return shards_by_channel(signal, *others)
    return shards_by_column(signal, *others)


def solution(mesh):
    return jax.shard_map(
        shards,
        mesh=mesh,
        in_specs=(P("seq", "ch", None), P("seq", "ch", None), P(), P(), P(), P()),
        out_specs=(P("seq", "ch", None), P("seq", "ch", None), P("seq", "ch"), P("seq", "ch")),
        check_vma=False,
    )
```

```python
import functools
import math

import jax
import jax.numpy as jnp
from jax import lax
from jax.experimental import pallas as pl
from jax.experimental.pallas import tpu as pltpu
from jax.sharding import PartitionSpec as P


def expand(blocks, width):
    tile = width // blocks.shape[0]
    return jnp.repeat(jnp.repeat(blocks, tile, axis=0), tile, axis=1)


def to_columns(rows, peers):
    rows_here, chans, width_two = rows.shape
    piece = width_two // peers
    arranged = rows.reshape(rows_here, chans, peers, piece).transpose(0, 2, 1, 3)
    return arranged.reshape(rows_here, peers, chans * piece)


def to_rows(received, chans):
    rows_here, peers, wide = received.shape
    piece = wide // chans
    arranged = received.reshape(rows_here, peers, chans, piece).transpose(0, 2, 1, 3)
    return arranged.reshape(rows_here, chans, peers * piece)


def shards_by_column(signal, cotangent, right_factor, left_factor, right_blocks, left_blocks):
    rows_here, chans, width_two = signal.shape
    width_one = left_factor.shape[0]
    peers = lax.axis_size("seq")
    right_mask = expand(right_blocks, width_two).astype(jnp.bfloat16)
    left_mask = expand(left_blocks, width_one).astype(jnp.bfloat16)
    right_eff = right_factor * right_mask
    left_eff = left_factor * left_mask
    flat_signal = signal.reshape(rows_here * chans, width_two)
    first_rows = jnp.dot(flat_signal, right_eff.T, preferred_element_type=jnp.float32)
    first_rows = to_columns(
        first_rows.astype(jnp.bfloat16).reshape(rows_here, chans, width_two), peers
    )
    sig_f = signal.astype(jnp.float32)
    gate = jax.nn.sigmoid(sig_f)
    swish = sig_f * gate
    cot_f = cotangent.astype(jnp.float32)
    grad_rows = to_columns((cot_f * swish).astype(jnp.bfloat16), peers)
    z_cols = lax.all_to_all(first_rows, "seq", split_axis=1, concat_axis=0, tiled=True)
    flat_cols = z_cols.reshape(width_one, z_cols.shape[2])
    result = jnp.dot(left_eff, flat_cols, preferred_element_type=jnp.float32)
    y_cols = result.astype(jnp.bfloat16).reshape(width_one, 1, z_cols.shape[2])
    y_back = lax.all_to_all(y_cols, "seq", split_axis=0, concat_axis=1, tiled=True)
    dy_cols = lax.all_to_all(grad_rows, "seq", split_axis=1, concat_axis=0, tiled=True)
    flat_cols = dy_cols.reshape(width_one, dy_cols.shape[2])
    result = lax.dot_general(
        left_eff, flat_cols, (((0,), (0,)), ((), ())), preferred_element_type=jnp.float32
    )
    dz_cols = result.astype(jnp.bfloat16).reshape(width_one, 1, dy_cols.shape[2])
    dz_back = lax.all_to_all(dz_cols, "seq", split_axis=0, concat_axis=1, tiled=True)
    y_rows = to_rows(y_back, chans)
    dz_rows = to_rows(dz_back, chans)
    y_f = y_rows.astype(jnp.float32)
    mixed = (sig_f + y_f * swish).astype(jnp.bfloat16)
    dz_flat = dz_rows.reshape(rows_here * chans, width_two)
    back = jnp.dot(dz_flat, right_eff, preferred_element_type=jnp.float32).reshape(
        rows_here, chans, width_two
    )
    dswish = gate * (1.0 + sig_f * (1.0 - gate))
    grad_signal = (cot_f * (1.0 + y_f * dswish) + back).astype(jnp.bfloat16)
    wide = z_cols.shape[2]
    z_flat = z_cols.reshape(width_one, wide)
    dy_flat = dy_cols.reshape(width_one, wide)
    left_term = lax.dot_general(
        dy_flat, z_flat, (((1,), (1,)), ((), ())), preferred_element_type=jnp.float32
    )
    right_term = lax.dot_general(
        dz_flat, flat_signal, (((0,), (0,)), ((), ())), preferred_element_type=jnp.float32
    )
    total_chans = chans * lax.axis_size("ch")
    right_term = right_term * right_mask.astype(jnp.float32) / math.sqrt(width_one * total_chans)
    left_term = left_term * left_mask.astype(jnp.float32) / math.sqrt(width_two * total_chans)
    partial_value = (
        lax.psum_scatter(right_term, "seq", scatter_dimension=0, tiled=True),
        lax.psum_scatter(left_term, "seq", scatter_dimension=0, tiled=True),
    )
    grad_right, grad_left = (
        lax.psum_scatter(partial_value[0], "ch", scatter_dimension=1, tiled=True),
        lax.psum_scatter(partial_value[1], "ch", scatter_dimension=1, tiled=True),
    )
    return (mixed, grad_signal, grad_right, grad_left)


def mix_kernel(
    peers, groups, parts, scales, right_blocks, left_blocks, xt, ct, right_in, left_in,
    mt, gt, out_r, out_l, right, left, left_t, grad_r, grad_l,
    xbuf, cbuf, zbuf, dybuf, dzbuf, pairs, staged, along, summed, across,
    send_sem, recv_sem, local_sem, pair_sems, along_sems, across_sems,
):
    me = lax.axis_index("seq")
    column = lax.axis_index("ch")
    rows = xt.shape[1]
    width = xt.shape[2]
    order = left.shape[0]
    tile = 256

    def own_rows(who):
        return pl.ds(pl.multiple_of(who * rows, rows), rows)

    def far(kind, part, source, target, who):
        return pltpu.make_async_remote_copy(
            src_ref=source,
            dst_ref=target,
            send_sem=send_sem.at[kind, part, who],
            recv_sem=recv_sem.at[kind, part, me],
            device_id=(who, column),
            device_id_type=pl.DeviceIdType.MESH,
        )

    def arrived(kind, part, source, target, who):
        return pltpu.make_async_remote_copy(
            src_ref=source,
            dst_ref=target,
            send_sem=send_sem.at[kind, part, who],
            recv_sem=recv_sem.at[kind, part, who],
            device_id=(who, column),
            device_id_type=pl.DeviceIdType.MESH,
        )

    def each_peer(action):
        @pl.loop(1, peers)
        def _(step):
            action(lax.rem(me + step, peers))

    barrier = pltpu.get_barrier_semaphore()

    def greet(who):
        pl.semaphore_signal(
            barrier, inc=1, device_id=(who, column), device_id_type=pl.DeviceIdType.MESH
        )

    each_peer(greet)

    @pl.loop(1, groups)
    def _(step):
        pl.semaphore_signal(
            barrier,
            inc=1,
            device_id=(me, lax.rem(column + step, groups)),
            device_id_type=pl.DeviceIdType.MESH,
        )

    pl.semaphore_wait(barrier, peers - 1 + groups - 1)

    inputs = ((0, xt, xbuf), (1, ct, cbuf))
    outputs = ((2, mt, xbuf), (3, gt, cbuf))

    def send_in(part):
        def one(who):
            for kind, source, held in inputs:
                far(kind, part, source.at[part * peers + who], held.at[part, own_rows(me)], who).start()

        each_peer(one)
        for kind, source, held in inputs:
            pltpu.make_async_copy(
                source.at[part * peers + me], held.at[part, own_rows(me)], local_sem.at[kind, part]
            ).start()

    def wait_in(part):
        def one(who):
            for kind, source, held in inputs:
                arrived(
                    kind, part, source.at[part * peers + who], held.at[part, own_rows(who)], who
                ).wait_recv()

        each_peer(one)
        for kind, source, held in inputs:
            pltpu.make_async_copy(
                source.at[part * peers + me], held.at[part, own_rows(me)], local_sem.at[kind, part]
            ).wait()

    def wait_in_sent(part):
        def one(who):
            for kind, source, held in inputs:
                far(kind, part, source.at[part * peers + who], held.at[part, own_rows(me)], who).wait_send()

        each_peer(one)

    def send_out(part):
        def one(who):
            for kind, target, held in outputs:
                far(kind, part, held.at[part, own_rows(who)], target.at[part * peers + me], who).start()

        each_peer(one)
        for kind, target, held in outputs:
            pltpu.make_async_copy(
                held.at[part, own_rows(me)], target.at[part * peers + me], local_sem.at[kind, part]
            ).start()

    def wait_out(part):
        def one(who):
            for kind, target, held in outputs:
                arrived(
                    kind, part, held.at[part, own_rows(who)], target.at[part * peers + who], who
                ).wait_recv()
                far(kind, part, held.at[part, own_rows(who)], target.at[part * peers + me], who).wait_send()

        each_peer(one)
        for kind, target, held in outputs:
            pltpu.make_async_copy(
                held.at[part, own_rows(me)], target.at[part * peers + me], local_sem.at[kind, part]
            ).wait()

    def at(step):
        return pl.ds(pl.multiple_of(step * tile, tile), tile)

    def dot(a, b, dims):
        return lax.dot_general(a, b, (dims, ((), ())), preferred_element_type=jnp.float32)

    def compute(part):
        @pl.loop(0, order // tile)
        def _(step):
            x = xbuf[part, at(step), :]
            zbuf[at(step), :] = dot(x, right[...], ((1,), (1,))).astype(jnp.bfloat16)
            sig = x.astype(jnp.float32)
            swish = sig * jax.nn.sigmoid(sig)
            cot = cbuf[part, at(step), :].astype(jnp.float32)
            dybuf[at(step), :] = (cot * swish).astype(jnp.bfloat16)

        @pl.loop(0, order // tile)
        def _(step):
            dzbuf[at(step), :] = dot(left_t[at(step), :], dybuf[...], ((1,), (0,))).astype(jnp.bfloat16)
            grad_l[at(step), :] += dot(dybuf[at(step), :], zbuf[...], ((1,), (1,)))

        @pl.loop(0, width // tile)
        def _(step):
            grad_r[at(step), :] += dot(dzbuf[:, at(step)], xbuf[part], ((0,), (0,)))

        @pl.loop(0, order // tile)
        def _(step):
            y = dot(left[at(step), :], zbuf[...], ((1,), (0,))).astype(jnp.bfloat16).astype(jnp.float32)
            back = dot(dzbuf[at(step), :], right[...], ((1,), (0,)))
            sig = xbuf[part, at(step), :].astype(jnp.float32)
            cot = cbuf[part, at(step), :].astype(jnp.float32)
            gate = jax.nn.sigmoid(sig)
            xbuf[part, at(step), :] = (sig + y * (sig * gate)).astype(jnp.bfloat16)
            dswish = gate * (1.0 + sig * (1.0 - gate))
            cbuf[part, at(step), :] = (cot * (1.0 + y * dswish) + back).astype(jnp.bfloat16)

    def apply_mask(source, blocks, target):
        side = source.shape[0] // blocks.shape[0]

        @pl.loop(0, blocks.shape[0])
        def _(down):
            here = pl.ds(pl.multiple_of(down * side, side), side)
            for right_of in range(blocks.shape[1]):
                there = slice(right_of * side, (right_of + 1) * side)
                keep = blocks[down, right_of].astype(jnp.float32)
                target[here, there] = (source[here, there].astype(jnp.float32) * keep).astype(jnp.bfloat16)

    half = peers // 2
    parity = lax.rem(me, 2)
    chip = me // 2
    sibling = me + 1 - 2 * parity
    cols = width // groups
    grads = ((0, grad_r), (1, grad_l))

    def between(source, target, sems, going, coming, who):
        return pltpu.make_async_remote_copy(
            src_ref=source,
            dst_ref=target,
            send_sem=sems.at[0, going[0], going[1]],
            recv_sem=sems.at[1, coming[0], coming[1]],
            device_id=who,
            device_id_type=pl.DeviceIdType.MESH,
        )

    def pair_copy(kind, grad, block):
        return between(
            grad.at[own_rows(2 * block + 1 - parity)], pairs.at[kind, block], pair_sems,
            (kind, block), (kind, block), (sibling, column),
        )

    def along_copy(kind, other, slot):
        return between(
            staged.at[kind, other], along.at[kind, slot], along_sems, (kind, other), (kind, slot), (me, other)
        )

    def across_copy(kind, other, slot):
        return between(
            summed.at[kind, other], across.at[kind, slot], across_sems,
            (kind, other), (kind, slot), (2 * other + parity, column),
        )

    def reduce_over_pairs():
        @pl.loop(0, half)
        def _(block):
            for kind, grad in grads:
                pair_copy(kind, grad, block).start()

        @pl.loop(0, half)
        def _(block):
            for kind, grad in grads:
                pair_copy(kind, grad, block).wait_recv()
                for line in range(groups):
                    there = slice(line * cols, (line + 1) * cols)
                    staged[kind, line, own_rows(block), :] = (
                        grad[own_rows(2 * block + parity), there] + pairs[kind, block, :, there]
                    )

    def send_along():
        @pl.loop(1, groups)
        def _(step):
            for kind in range(2):
                along_copy(kind, lax.rem(column + step, groups), column).start()

    def finish_sums():
        @pl.loop(1, groups)
        def _(step):
            other = lax.rem(column + step, groups)
            for kind in range(2):
                along_copy(kind, other, other).wait_recv()

        @pl.loop(0, half)
        def _(block):
            for kind in range(2):
                total = staged[kind, column, own_rows(block), :]
                for step in range(1, groups):
                    total = total + along[kind, lax.rem(column + step, groups), own_rows(block), :]
                summed[kind, block] = total

        @pl.loop(1, half)
        def _(step):
            for kind in range(2):
                across_copy(kind, lax.rem(chip + step, half), chip).start()

        @pl.loop(1, half)
        def _(step):
            other = lax.rem(chip + step, half)
            for kind in range(2):
                across_copy(kind, other, other).wait_recv()

        for kind, out, blocks in ((0, out_r, right_blocks), (1, out_l, left_blocks)):
            side = width // blocks.shape[0]
            total = summed[kind, chip]
            for step in range(1, half):
                total = total + across[kind, lax.rem(chip + step, half)]
            for right_of in range(cols // side):
                there = slice(right_of * side, (right_of + 1) * side)
                keep = blocks[me * rows // side, column * (cols // side) + right_of].astype(jnp.float32)
                out[:, there] = total[:, there] * keep / scales[kind]

        @pl.loop(0, half)
        def _(block):
            for kind, grad in grads:
                pair_copy(kind, grad, block).wait_send()

        @pl.loop(1, groups)
        def _(step):
            for kind in range(2):
                along_copy(kind, lax.rem(column + step, groups), column).wait_send()

        @pl.loop(1, half)
        def _(step):
            for kind in range(2):
                across_copy(kind, lax.rem(chip + step, half), chip).wait_send()

    send_in(0)
    if parts > 1:
        send_in(1)
    grad_r[...] = jnp.zeros_like(grad_r)
    grad_l[...] = jnp.zeros_like(grad_l)
    apply_mask(right_in, right_blocks, right)
    apply_mask(left_in, left_blocks, left)

    @pl.loop(0, order // tile)
    def _(step):
        left_t[at(step), :] = left[:, at(step)].T

    @pl.loop(0, parts)
    def _(part):
        wait_in(part)

        @pl.when(part + 2 < parts)
        def _():
            send_in(part + 2)

        compute(part)

        @pl.when(part + 1 < parts)
        def _():
            send_out(part)

    reduce_over_pairs()
    send_along()
    send_out(parts - 1)
    finish_sums()

    @pl.loop(0, parts)
    def _(part):
        wait_in_sent(part)
        wait_out(part)


def shards_by_channel(signal, cotangent, right_factor, left_factor, right_blocks, left_blocks):
    rows_here, chans, width_two = signal.shape
    width_one = left_factor.shape[0]
    peers = lax.axis_size("seq")
    groups = lax.axis_size("ch")
    parts = chans // peers
    xt = signal.transpose(1, 0, 2)
    ct = cotangent.transpose(1, 0, 2)
    half = peers // 2
    cols = width_two // groups
    square = (width_one, width_two)
    block = jax.ShapeDtypeStruct((rows_here, cols), jnp.float32)
    scales = (math.sqrt(width_one * chans * groups), math.sqrt(width_two * chans * groups))
    hbm = pl.BlockSpec(memory_space=pl.ANY)
    vmem = pl.BlockSpec(memory_space=pltpu.VMEM)
    smem = pl.BlockSpec(memory_space=pltpu.SMEM)
    mt, gt, grad_right, grad_left = pl.pallas_call(
        functools.partial(mix_kernel, peers, groups, parts, scales),
        out_shape=(
            jax.ShapeDtypeStruct(xt.shape, jnp.bfloat16),
            jax.ShapeDtypeStruct(xt.shape, jnp.bfloat16),
            block,
            block,
        ),
        in_specs=[smem, smem, hbm, hbm, vmem, vmem],
        out_specs=(hbm, hbm, vmem, vmem),
        scratch_shapes=[
            pltpu.VMEM(square, jnp.bfloat16),
            pltpu.VMEM(square, jnp.bfloat16),
            pltpu.VMEM(square, jnp.bfloat16),
            pltpu.VMEM(square, jnp.float32),
            pltpu.VMEM(square, jnp.float32),
            pltpu.VMEM((parts, *square), jnp.bfloat16),
            pltpu.VMEM((parts, *square), jnp.bfloat16),
            pltpu.VMEM(square, jnp.bfloat16),
            pltpu.VMEM(square, jnp.bfloat16),
            pltpu.VMEM(square, jnp.bfloat16),
            pltpu.VMEM((2, half, rows_here, width_two), jnp.float32),
            pltpu.VMEM((2, groups, half * rows_here, cols), jnp.float32),
            pltpu.VMEM((2, groups, half * rows_here, cols), jnp.float32),
            pltpu.VMEM((2, half, rows_here, cols), jnp.float32),
            pltpu.VMEM((2, half, rows_here, cols), jnp.float32),
            pltpu.SemaphoreType.DMA((4, parts, peers)),
            pltpu.SemaphoreType.DMA((4, parts, peers)),
            pltpu.SemaphoreType.DMA((4, parts)),
            pltpu.SemaphoreType.DMA((2, 2, half)),
            pltpu.SemaphoreType.DMA((2, 2, groups)),
            pltpu.SemaphoreType.DMA((2, 2, half)),
        ],
        compiler_params=pltpu.CompilerParams(
            collective_id=0, has_side_effects=True, vmem_limit_bytes=60 * 2**20
        ),
    )(right_blocks, left_blocks, xt, ct, right_factor, left_factor)
    return (mt.transpose(1, 0, 2), gt.transpose(1, 0, 2), grad_right, grad_left)


def shards(signal, *others):
    rows_here, chans, width_two = signal.shape
    peers = lax.axis_size("seq")
    width_one = others[1].shape[0]
    sides = (width_two // others[3].shape[0], width_one // others[4].shape[0])
    fits = chans % peers == 0 and rows_here % 16 == 0 and peers % 2 == 0
    fits = fits and sides == (128, 128) and rows_here == 128
    fits = fits and width_two // lax.axis_size("ch") % 128 == 0
    if fits and width_one == 1024 and width_two == 1024 and chans // peers <= 4:
        return shards_by_channel(signal, *others)
    return shards_by_column(signal, *others)


def solution(mesh):
    return jax.shard_map(
        shards,
        mesh=mesh,
        in_specs=(P("seq", "ch", None), P("seq", "ch", None), P(), P(), P(), P()),
        out_specs=(P("seq", "ch", None), P("seq", "ch", None), P("seq", "ch"), P("seq", "ch")),
        check_vma=False,
    )
```

```python
import functools
import math

import jax
import jax.numpy as jnp
from jax import lax
from jax.experimental import pallas as pl
from jax.experimental.pallas import tpu as pltpu
from jax.sharding import PartitionSpec as P


def expand(blocks, width):
    tile = width // blocks.shape[0]
    return jnp.repeat(jnp.repeat(blocks, tile, axis=0), tile, axis=1)


def to_columns(rows, peers):
    rows_here, chans, width_two = rows.shape
    piece = width_two // peers
    arranged = rows.reshape(rows_here, chans, peers, piece).transpose(0, 2, 1, 3)
    return arranged.reshape(rows_here, peers, chans * piece)


def to_rows(received, chans):
    rows_here, peers, wide = received.shape
    piece = wide // chans
    arranged = received.reshape(rows_here, peers, chans, piece).transpose(0, 2, 1, 3)
    return arranged.reshape(rows_here, chans, peers * piece)


def shards_by_column(signal, cotangent, right_factor, left_factor, right_blocks, left_blocks):
    rows_here, chans, width_two = signal.shape
    width_one = left_factor.shape[0]
    peers = lax.axis_size("seq")
    right_mask = expand(right_blocks, width_two).astype(jnp.bfloat16)
    left_mask = expand(left_blocks, width_one).astype(jnp.bfloat16)
    right_eff = right_factor * right_mask
    left_eff = left_factor * left_mask
    flat_signal = signal.reshape(rows_here * chans, width_two)
    first_rows = jnp.dot(flat_signal, right_eff.T, preferred_element_type=jnp.float32)
    first_rows = to_columns(
        first_rows.astype(jnp.bfloat16).reshape(rows_here, chans, width_two), peers
    )
    sig_f = signal.astype(jnp.float32)
    gate = jax.nn.sigmoid(sig_f)
    swish = sig_f * gate
    cot_f = cotangent.astype(jnp.float32)
    grad_rows = to_columns((cot_f * swish).astype(jnp.bfloat16), peers)
    z_cols = lax.all_to_all(first_rows, "seq", split_axis=1, concat_axis=0, tiled=True)
    flat_cols = z_cols.reshape(width_one, z_cols.shape[2])
    result = jnp.dot(left_eff, flat_cols, preferred_element_type=jnp.float32)
    y_cols = result.astype(jnp.bfloat16).reshape(width_one, 1, z_cols.shape[2])
    y_back = lax.all_to_all(y_cols, "seq", split_axis=0, concat_axis=1, tiled=True)
    dy_cols = lax.all_to_all(grad_rows, "seq", split_axis=1, concat_axis=0, tiled=True)
    flat_cols = dy_cols.reshape(width_one, dy_cols.shape[2])
    result = lax.dot_general(
        left_eff, flat_cols, (((0,), (0,)), ((), ())), preferred_element_type=jnp.float32
    )
    dz_cols = result.astype(jnp.bfloat16).reshape(width_one, 1, dy_cols.shape[2])
    dz_back = lax.all_to_all(dz_cols, "seq", split_axis=0, concat_axis=1, tiled=True)
    y_rows = to_rows(y_back, chans)
    dz_rows = to_rows(dz_back, chans)
    y_f = y_rows.astype(jnp.float32)
    mixed = (sig_f + y_f * swish).astype(jnp.bfloat16)
    dz_flat = dz_rows.reshape(rows_here * chans, width_two)
    back = jnp.dot(dz_flat, right_eff, preferred_element_type=jnp.float32).reshape(
        rows_here, chans, width_two
    )
    dswish = gate * (1.0 + sig_f * (1.0 - gate))
    grad_signal = (cot_f * (1.0 + y_f * dswish) + back).astype(jnp.bfloat16)
    wide = z_cols.shape[2]
    z_flat = z_cols.reshape(width_one, wide)
    dy_flat = dy_cols.reshape(width_one, wide)
    left_term = lax.dot_general(
        dy_flat, z_flat, (((1,), (1,)), ((), ())), preferred_element_type=jnp.float32
    )
    right_term = lax.dot_general(
        dz_flat, flat_signal, (((0,), (0,)), ((), ())), preferred_element_type=jnp.float32
    )
    total_chans = chans * lax.axis_size("ch")
    right_term = right_term * right_mask.astype(jnp.float32) / math.sqrt(width_one * total_chans)
    left_term = left_term * left_mask.astype(jnp.float32) / math.sqrt(width_two * total_chans)
    partial_value = (
        lax.psum_scatter(right_term, "seq", scatter_dimension=0, tiled=True),
        lax.psum_scatter(left_term, "seq", scatter_dimension=0, tiled=True),
    )
    grad_right, grad_left = (
        lax.psum_scatter(partial_value[0], "ch", scatter_dimension=1, tiled=True),
        lax.psum_scatter(partial_value[1], "ch", scatter_dimension=1, tiled=True),
    )
    return (mixed, grad_signal, grad_right, grad_left)


def mix_kernel(
    peers, groups, parts, scales, right_blocks, left_blocks, signal, cotangent, right_in, left_in,
    mt, gt, out_r, out_l, right, left, grad_r, grad_l,
    xbuf, cbuf, zbuf, dybuf, dzbuf, pairs, along, summed, across, slab, turned,
    send_sem, recv_sem, local_sem, pair_sems, along_sems, across_sems, load_sem,
):
    me = lax.axis_index("seq")
    column = lax.axis_index("ch")
    rows = signal.shape[0]
    width = signal.shape[2]
    order = left.shape[0]
    tile = 256

    def own_rows(who):
        return pl.ds(pl.multiple_of(who * rows, rows), rows)

    def far(kind, part, source, target, who):
        return pltpu.make_async_remote_copy(
            src_ref=source,
            dst_ref=target,
            send_sem=send_sem.at[kind, part, who],
            recv_sem=recv_sem.at[kind, part, me],
            device_id=(who, column),
            device_id_type=pl.DeviceIdType.MESH,
        )

    def arrived(kind, part, source, target, who):
        return pltpu.make_async_remote_copy(
            src_ref=source,
            dst_ref=target,
            send_sem=send_sem.at[kind, part, who],
            recv_sem=recv_sem.at[kind, part, who],
            device_id=(who, column),
            device_id_type=pl.DeviceIdType.MESH,
        )

    def each_peer(action):
        @pl.loop(1, peers)
        def _(step):
            action(lax.rem(me + step, peers))

    barrier = pltpu.get_barrier_semaphore()
    pltpu.make_async_copy(signal.at[:, pl.ds(0, peers), :], slab, load_sem.at[0]).start()

    def greet(who):
        pl.semaphore_signal(
            barrier, inc=1, device_id=(who, column), device_id_type=pl.DeviceIdType.MESH
        )

    each_peer(greet)

    @pl.loop(1, groups)
    def _(step):
        pl.semaphore_signal(
            barrier,
            inc=1,
            device_id=(me, lax.rem(column + step, groups)),
            device_id_type=pl.DeviceIdType.MESH,
        )

    pl.semaphore_wait(barrier, peers - 1 + groups - 1)

    inputs = ((0, signal, xbuf), (1, cotangent, cbuf))
    outputs = ((2, mt, xbuf), (3, gt, cbuf))

    def load(part, kind, source):
        there = pl.ds(pl.multiple_of(part * peers, peers), peers)
        return pltpu.make_async_copy(source.at[:, there, :], slab, load_sem.at[kind])

    def start_loads(part):
        load(part, 0, signal).start()

    def in_copy(kind, part, held, who):
        return far(kind, part, turned.at[lax.rem(part, 2), kind, who], held.at[part, own_rows(me)], who)

    def own_copy(kind, part, held):
        return pltpu.make_async_copy(
            turned.at[lax.rem(part, 2), kind, me], held.at[part, own_rows(me)], local_sem.at[kind, part]
        )

    def send_in(part):
        for kind, source, held in inputs:
            load(part, kind, source).wait()

            @pl.loop(0, rows // 16)
            def _(step):
                here = pl.ds(pl.multiple_of(step * 16, 16), 16)
                turned[lax.rem(part, 2), kind, :, here, :] = jnp.swapaxes(slab[here], 0, 1)

            if kind == 0:
                load(part, 1, cotangent).start()

            each_peer(lambda who: in_copy(kind, part, held, who).start())
            own_copy(kind, part, held).start()

    def wait_in(part):
        def one(who):
            for kind, source, held in inputs:
                arrived(
                    kind, part, turned.at[lax.rem(part, 2), kind, who], held.at[part, own_rows(who)], who
                ).wait_recv()

        each_peer(one)
        for kind, source, held in inputs:
            own_copy(kind, part, held).wait()

    def wait_in_sent(part):
        def one(who):
            for kind, source, held in inputs:
                in_copy(kind, part, held, who).wait_send()

        each_peer(one)

    def send_out(part):
        def one(who):
            for kind, target, held in outputs:
                far(kind, part, held.at[part, own_rows(who)], target.at[part * peers + me], who).start()

        each_peer(one)
        for kind, target, held in outputs:
            pltpu.make_async_copy(
                held.at[part, own_rows(me)], target.at[part * peers + me], local_sem.at[kind, part]
            ).start()

    def wait_out(part):
        def one(who):
            for kind, target, held in outputs:
                arrived(
                    kind, part, held.at[part, own_rows(who)], target.at[part * peers + who], who
                ).wait_recv()
                far(kind, part, held.at[part, own_rows(who)], target.at[part * peers + me], who).wait_send()

        each_peer(one)
        for kind, target, held in outputs:
            pltpu.make_async_copy(
                held.at[part, own_rows(me)], target.at[part * peers + me], local_sem.at[kind, part]
            ).wait()

    def at(step):
        return pl.ds(pl.multiple_of(step * tile, tile), tile)

    def dot(a, b, dims):
        return lax.dot_general(a, b, (dims, ((), ())), preferred_element_type=jnp.float32)

    def compute(part):
        @pl.loop(0, order // tile)
        def _(step):
            x = xbuf[part, at(step), :]
            zbuf[at(step), :] = dot(x, right[...], ((1,), (1,))).astype(jnp.bfloat16)
            sig = x.astype(jnp.float32)
            swish = sig * jax.nn.sigmoid(sig)
            cot = cbuf[part, at(step), :].astype(jnp.float32)
            dybuf[at(step), :] = (cot * swish).astype(jnp.bfloat16)

        @pl.loop(0, order // tile)
        def _(step):
            dzbuf[at(step), :] = dot(left[:, at(step)], dybuf[...], ((0,), (0,))).astype(jnp.bfloat16)
            grad_l[at(step), :] += dot(dybuf[at(step), :], zbuf[...], ((1,), (1,)))

        @pl.loop(0, width // tile)
        def _(step):
            grad_r[at(step), :] += dot(dzbuf[:, at(step)], xbuf[part], ((0,), (0,)))

        @pl.loop(0, order // tile)
        def _(step):
            y = dot(left[at(step), :], zbuf[...], ((1,), (0,))).astype(jnp.bfloat16).astype(jnp.float32)
            back = dot(dzbuf[at(step), :], right[...], ((1,), (0,)))
            sig = xbuf[part, at(step), :].astype(jnp.float32)
            cot = cbuf[part, at(step), :].astype(jnp.float32)
            gate = jax.nn.sigmoid(sig)
            xbuf[part, at(step), :] = (sig + y * (sig * gate)).astype(jnp.bfloat16)
            dswish = gate * (1.0 + sig * (1.0 - gate))
            cbuf[part, at(step), :] = (cot * (1.0 + y * dswish) + back).astype(jnp.bfloat16)

    def apply_mask(blocks, target):
        side = target.shape[0] // blocks.shape[0]

        @pl.loop(0, blocks.shape[0])
        def _(down):
            here = pl.ds(pl.multiple_of(down * side, side), side)
            for right_of in range(blocks.shape[1]):
                there = slice(right_of * side, (right_of + 1) * side)
                keep = blocks[down, right_of].astype(jnp.float32)
                target[here, there] = (target[here, there].astype(jnp.float32) * keep).astype(jnp.bfloat16)

    half = peers // 2
    parity = lax.rem(me, 2)
    chip = me // 2
    sibling = me + 1 - 2 * parity
    cols = width // groups
    grads = ((0, grad_r), (1, grad_l))

    def between(source, target, sems, going, coming, who):
        return pltpu.make_async_remote_copy(
            src_ref=source,
            dst_ref=target,
            send_sem=sems.at[0, going[0], going[1]],
            recv_sem=sems.at[1, coming[0], coming[1]],
            device_id=who,
            device_id_type=pl.DeviceIdType.MESH,
        )

    def pair_copy(kind, grad, block):
        return between(
            grad.at[own_rows(2 * block + 1 - parity)], pairs.at[kind, block], pair_sems,
            (kind, block), (kind, block), (sibling, column),
        )

    def own_cols(line):
        return pl.ds(pl.multiple_of(line * cols, cols), cols)

    def along_copy(kind, grad, other, slot, block):
        return pltpu.make_async_remote_copy(
            src_ref=grad.at[own_rows(2 * block + parity), own_cols(other)],
            dst_ref=along.at[kind, slot, own_rows(block)],
            send_sem=along_sems.at[0, kind, other, block],
            recv_sem=along_sems.at[1, kind, slot, block],
            device_id=(me, other),
            device_id_type=pl.DeviceIdType.MESH,
        )

    def across_copy(kind, other, slot):
        return between(
            summed.at[kind, other], across.at[kind, slot], across_sems,
            (kind, other), (kind, slot), (2 * other + parity, column),
        )

    def reduce_over_pairs():
        @pl.loop(0, half)
        def _(block):
            for kind, grad in grads:
                pair_copy(kind, grad, block).start()

        @pl.loop(0, half)
        def _(block):
            for kind, grad in grads:
                pair_copy(kind, grad, block).wait_recv()
                grad[own_rows(2 * block + parity), :] += pairs[kind, block]

    def send_along():
        @pl.loop(1, groups)
        def _(step):
            for block in range(half):
                for kind, grad in grads:
                    along_copy(kind, grad, lax.rem(column + step, groups), column, block).start()

    def finish_sums():
        @pl.loop(1, groups)
        def _(step):
            other = lax.rem(column + step, groups)
            for block in range(half):
                for kind, grad in grads:
                    along_copy(kind, grad, other, other, block).wait_recv()

        @pl.loop(0, half)
        def _(block):
            for kind, grad in grads:
                total = grad[own_rows(2 * block + parity), own_cols(column)]
                for step in range(1, groups):
                    total = total + along[kind, lax.rem(column + step, groups), own_rows(block), :]
                summed[kind, block] = total

        @pl.loop(1, half)
        def _(step):
            for kind in range(2):
                across_copy(kind, lax.rem(chip + step, half), chip).start()

        @pl.loop(1, half)
        def _(step):
            other = lax.rem(chip + step, half)
            for kind in range(2):
                across_copy(kind, other, other).wait_recv()

        for kind, out, blocks in ((0, out_r, right_blocks), (1, out_l, left_blocks)):
            side = width // blocks.shape[0]
            total = summed[kind, chip]
            for step in range(1, half):
                total = total + across[kind, lax.rem(chip + step, half)]
            for right_of in range(cols // side):
                there = slice(right_of * side, (right_of + 1) * side)
                keep = blocks[me * rows // side, column * (cols // side) + right_of].astype(jnp.float32)
                out[:, there] = total[:, there] * keep / scales[kind]

        @pl.loop(0, half)
        def _(block):
            for kind, grad in grads:
                pair_copy(kind, grad, block).wait_send()

        @pl.loop(1, groups)
        def _(step):
            for block in range(half):
                for kind, grad in grads:
                    along_copy(kind, grad, lax.rem(column + step, groups), column, block).wait_send()

        @pl.loop(1, half)
        def _(step):
            for kind in range(2):
                across_copy(kind, lax.rem(chip + step, half), chip).wait_send()

    fetched = (
        pltpu.make_async_copy(right_in, right, load_sem.at[2]),
        pltpu.make_async_copy(left_in, left, load_sem.at[3]),
    )
    send_in(0)
    if parts > 1:
        start_loads(1)
    for copy in fetched:
        copy.start()
    if parts > 1:
        send_in(1)
    if parts > 2:
        start_loads(2)
    for copy in fetched:
        copy.wait()
    grad_r[...] = jnp.zeros_like(grad_r)
    grad_l[...] = jnp.zeros_like(grad_l)
    apply_mask(right_blocks, right)
    apply_mask(left_blocks, left)

    @pl.loop(0, parts)
    def _(part):
        wait_in(part)

        @pl.when(part + 2 < parts)
        def _():
            wait_in_sent(part)
            send_in(part + 2)

        @pl.when(part + 3 < parts)
        def _():
            start_loads(part + 3)

        compute(part)

        @pl.when(part + 1 < parts)
        def _():
            send_out(part)

    reduce_over_pairs()
    send_along()
    send_out(parts - 1)
    finish_sums()

    @pl.loop(0, parts)
    def _(part):
        @pl.when(part + 2 >= parts)
        def _():
            wait_in_sent(part)

        wait_out(part)


def turn_kernel(source, target):
    target[...] = jnp.swapaxes(source[...], 0, 1)


def turn_back(array):
    chans, rows, width = array.shape
    step = 16
    return pl.pallas_call(
        turn_kernel,
        grid=(rows // step,),
        out_shape=jax.ShapeDtypeStruct((rows, chans, width), array.dtype),
        in_specs=[pl.BlockSpec((chans, step, width), lambda place: (0, place, 0))],
        out_specs=pl.BlockSpec((step, chans, width), lambda place: (place, 0, 0)),
        compiler_params=pltpu.CompilerParams(vmem_limit_bytes=16 * 2**20),
    )(array)


def shards_by_channel(signal, cotangent, right_factor, left_factor, right_blocks, left_blocks):
    rows_here, chans, width_two = signal.shape
    width_one = left_factor.shape[0]
    peers = lax.axis_size("seq")
    groups = lax.axis_size("ch")
    parts = chans // peers
    turned = jax.ShapeDtypeStruct((chans, rows_here, width_two), jnp.bfloat16)
    half = peers // 2
    cols = width_two // groups
    square = (width_one, width_two)
    block = jax.ShapeDtypeStruct((rows_here, cols), jnp.float32)
    scales = (math.sqrt(width_one * chans * groups), math.sqrt(width_two * chans * groups))
    hbm = pl.BlockSpec(memory_space=pl.ANY)
    vmem = pl.BlockSpec(memory_space=pltpu.VMEM)
    smem = pl.BlockSpec(memory_space=pltpu.SMEM)
    mt, gt, grad_right, grad_left = pl.pallas_call(
        functools.partial(mix_kernel, peers, groups, parts, scales),
        out_shape=(
            turned,
            turned,
            block,
            block,
        ),
        in_specs=[smem, smem, hbm, hbm, hbm, hbm],
        out_specs=(hbm, hbm, vmem, vmem),
        scratch_shapes=[
            pltpu.VMEM(square, jnp.bfloat16),
            pltpu.VMEM(square, jnp.bfloat16),
            pltpu.VMEM(square, jnp.float32),
            pltpu.VMEM(square, jnp.float32),
            pltpu.VMEM((parts, *square), jnp.bfloat16),
            pltpu.VMEM((parts, *square), jnp.bfloat16),
            pltpu.VMEM(square, jnp.bfloat16),
            pltpu.VMEM(square, jnp.bfloat16),
            pltpu.VMEM(square, jnp.bfloat16),
            pltpu.VMEM((2, half, rows_here, width_two), jnp.float32),
            pltpu.VMEM((2, groups, half * rows_here, cols), jnp.float32),
            pltpu.VMEM((2, half, rows_here, cols), jnp.float32),
            pltpu.VMEM((2, half, rows_here, cols), jnp.float32),
            pltpu.VMEM((rows_here, peers, width_two), jnp.bfloat16),
            pltpu.VMEM((2, 2, peers, rows_here, width_two), jnp.bfloat16),
            pltpu.SemaphoreType.DMA((4, parts, peers)),
            pltpu.SemaphoreType.DMA((4, parts, peers)),
            pltpu.SemaphoreType.DMA((4, parts)),
            pltpu.SemaphoreType.DMA((2, 2, half)),
            pltpu.SemaphoreType.DMA((2, 2, groups, half)),
            pltpu.SemaphoreType.DMA((2, 2, half)),
            pltpu.SemaphoreType.DMA((4,)),
        ],
        compiler_params=pltpu.CompilerParams(
            collective_id=0, has_side_effects=True, vmem_limit_bytes=60 * 2**20
        ),
    )(right_blocks, left_blocks, signal, cotangent, right_factor, left_factor)
    return (turn_back(mt), turn_back(gt), grad_right, grad_left)


def shards(signal, *others):
    rows_here, chans, width_two = signal.shape
    peers = lax.axis_size("seq")
    width_one = others[1].shape[0]
    sides = (width_two // others[3].shape[0], width_one // others[4].shape[0])
    fits = chans % peers == 0 and rows_here % 16 == 0 and peers % 2 == 0
    fits = fits and sides == (128, 128) and rows_here == 128
    fits = fits and width_two // lax.axis_size("ch") % 128 == 0
    if fits and width_one == 1024 and width_two == 1024 and chans // peers <= 4:
        return shards_by_channel(signal, *others)
    return shards_by_column(signal, *others)


def solution(mesh):
    return jax.shard_map(
        shards,
        mesh=mesh,
        in_specs=(P("seq", "ch", None), P("seq", "ch", None), P(), P(), P(), P()),
        out_specs=(P("seq", "ch", None), P("seq", "ch", None), P("seq", "ch"), P("seq", "ch")),
        check_vma=False,
    )
```
